32 devices in a mesh: dp: 4 (over y, x), owner: 8 (over z, core).
Axes of the slice: x: 2, y: 2, z: 4, core: 2. Of those that a mesh axis runs over, the one named last changes fastest.
Arguments:
- sample_rows: bfloat16 [49152, 4096], P(('dp', 'owner')), may hold values from -60 to 60
- start_basis: bfloat16 [4096, 128], P(('dp', 'owner')), may hold values from -0.09375 to 0.09375
Outputs:
- projected: bfloat16 [49152, 128], P(('dp', 'owner'))
- basis: float32 [4096, 128], P(('dp', 'owner'))
The draws below stay inside these ranges and needn't reach their ends.
All inputs are finite; a program needn't handle non-finite values.
Results may differ from the reference program's by a relative error of at most 0.0056.
Values may be sent and summed in bfloat16 or wider, within the bound.
No kernel may reach another device: no remote copies, remote signals or barrier semaphores. Data moves between devices by JAX's collectives and lax.ppermute only.
A program may use at most 64 MiB of HBM per device.

```python
import math
import jax
import jax.numpy as jnp
from jax import lax

D = 4096
K = 128
ITERS = 2
ROWS = 49152


def draw_sample_rows(key, part):
    first_key = jax.random.fold_in(key, 11)
    second_key = jax.random.fold_in(key, 12)
    third_key = jax.random.fold_in(key, 13)
    values = jnp.clip(jax.random.normal(first_key, (ROWS, D), jnp.float32), -4.0, 4.0)
    columns = jax.random.uniform(third_key, (1, D), jnp.float32, 0.5, 1.5)
    scales = jnp.exp(jax.random.uniform(second_key, (ROWS, 1), jnp.float32, jnp.log(0.3), jnp.log(3.0)))
    rising = 1.0 + 2.0 * jnp.arange(ROWS, dtype=jnp.float32)[:, None] / ROWS
    return (values * scales * rising * columns).astype(jnp.bfloat16)


def shard_levels(rng, shape, cuts, least, largest):
    level = 1.0
    for dim, blocks in cuts:
        steps = jax.random.uniform(jax.random.fold_in(jax.random.fold_in(rng, 6), dim), (blocks,), jnp.float32, least / len(cuts), largest / len(cuts))
        level = level * jnp.repeat(jnp.exp(steps), shape[dim] // blocks).reshape((-1,) + (1,) * (len(shape) - 1 - dim))
    return level


def noise(rng, extent, deviation, bound, split=(), held_as=jnp.bfloat16):
    entries = deviation * jax.random.normal(rng, extent, jnp.float32)
    if split:
        entries = entries * shard_levels(rng, extent, split, -0.22, 0.18)
    return jnp.clip(entries, -bound, bound).astype(held_as)


def setup_inputs(seed: int = 0) -> dict:
    arg_keys = jax.random.split(jax.random.key(seed), 3)
    return {
        "sample_rows": draw_sample_rows(jax.random.fold_in(arg_keys[2], 71), 0),
        "start_basis": noise(arg_keys[1], (D, K), D ** -0.5, 0.09375, ((0, 32),)),
    }


def reference(sample_rows, start_basis):
    current = start_basis
    image = jnp.dot(sample_rows.astype(jnp.float32), current.astype(jnp.float32), preferred_element_type=jnp.float32)
    ortho = jnp.zeros((D, K), jnp.float32)
    for iteration in range(ITERS):
        image_low = image.astype(jnp.bfloat16)
        sketch = lax.dot_general(sample_rows.astype(jnp.float32), image_low.astype(jnp.float32), (((0,), (0,)), ((), ())), preferred_element_type=jnp.float32)
        gram = lax.dot_general(sketch.astype(jnp.float32), sketch.astype(jnp.float32), (((0,), (0,)), ((), ())), precision=lax.Precision.HIGHEST, preferred_element_type=jnp.float32)
        lower = jnp.linalg.cholesky(gram)
        ortho = jax.scipy.linalg.solve_triangular(lower, sketch.T, lower=True).T
        current = ortho.astype(jnp.bfloat16)
        image = jnp.dot(sample_rows.astype(jnp.float32), current.astype(jnp.float32), preferred_element_type=jnp.float32)
    return (image.astype(jnp.bfloat16), ortho * math.sqrt(D))
```

```python
import functools
import math

import jax
import jax.numpy as jnp
from jax import lax
from jax.experimental import pallas as pl
from jax.experimental.pallas import tpu as pltpu
from jax.sharding import PartitionSpec as P

ITERS = 2
F32 = jnp.float32
BF16 = jnp.bfloat16


def digits(size, stride):
    found = []
    while size > 1:
        radix = 4 if size % 4 == 0 else 2
        found.append((stride, radix))
        size //= radix
        stride *= radix
    return found


class Plan:
    def __init__(self, mesh):
        self.axes = tuple(mesh.axis_names)
        outer, inner = (mesh.shape[a] for a in self.axes)
        self.n = outer * inner
        assert self.n & (self.n - 1) == 0 and inner % 2 == 0
        self.steps = digits(outer, inner) + digits(inner // 2, 2)[::-1]
        masks = [0]
        for stride, radix in self.steps:
            masks = [m ^ (stride * d) for m in masks for d in range(radix)]
        self.masks = masks

    def swap(self, x, mask):
        return lax.ppermute(x, self.axes, [(i, i ^ mask) for i in range(self.n)])

    def reduce_scatter(self, own, other):
        total = own + self.swap(other, 1).astype(F32)
        for stride, radix in self.steps:
            parts = total.reshape((radix, -1) + total.shape[1:])
            received = [self.swap(parts[d].astype(BF16), stride * d) for d in range(1, radix)]
            total = parts[0]
            for r in received:
                total = total + r.astype(F32)
        return total[0]

    def all_gather(self, block):
        have = block[None]
        for stride, radix in self.steps[::-1]:
            have = jnp.concatenate([have] + [self.swap(have, stride * d) for d in range(1, radix)], 0)
        return have, self.swap(have, 1)


def row_tile(rows):
    return 256 if rows % 256 == 0 else rows


def assemble(masks, me, near_ref, far_ref, full_ref):
    block = near_ref.shape[1]
    for slot, mask in enumerate(masks):
        at = jnp.bitwise_xor(me, mask)
        full_ref[pl.ds(pl.multiple_of(at * block, block), block), :] = near_ref[slot]
        at = jnp.bitwise_xor(me, mask ^ 1)
        full_ref[pl.ds(pl.multiple_of(at * block, block), block), :] = far_ref[slot]


def sketch_kernel(masks, scaled, me_ref, a_ref, near_ref, far_ref, *refs):
    if scaled:
        inv_ref, own_ref, other_ref, full_ref, acc_ref, turned_ref = refs
    else:
        own_ref, other_ref, full_ref, acc_ref, turned_ref = refs
    step = pl.program_id(0)
    me = me_ref[0]

    @pl.when(step == 0)
    def _():
        assemble(masks, me, near_ref, far_ref, full_ref)

    tile = a_ref[...]
    image = jnp.dot(tile, full_ref[...], preferred_element_type=F32)
    if scaled:
        image = jnp.dot(image, inv_ref[...], precision=lax.Precision.HIGHEST, preferred_element_type=F32)
    low = image.astype(BF16)
    term = lax.dot_general(low, tile, (((0,), (0,)), ((), ())), preferred_element_type=F32)

    @pl.when(step == 0)
    def _():
        acc_ref[...] = term

    @pl.when(step > 0)
    def _():
        acc_ref[...] += term

    @pl.when(step == pl.num_programs(0) - 1)
    def _():
        turned_ref[...] = acc_ref[...].T
        block = own_ref.shape[1]
        for slot, mask in enumerate(masks):
            at = jnp.bitwise_xor(me, mask)
            own_ref[slot] = turned_ref[pl.ds(pl.multiple_of(at * block, block), block), :]
            at = jnp.bitwise_xor(me, mask ^ 1)
            other_ref[slot] = turned_ref[pl.ds(pl.multiple_of(at * block, block), block), :].astype(BF16)


def sketch_call(masks, me, a, near, far, inverse=None):
    rows, features = a.shape
    slots, block, rank = near.shape
    tile = row_tile(rows)
    whole = lambda shape: pl.BlockSpec(shape, lambda i, *_: (0,) * len(shape))
    given = [a, near, far] + ([] if inverse is None else [inverse])
    specs = [pl.BlockSpec((tile, features), lambda i, *_: (i, 0)), whole(near.shape), whole(far.shape)]
    if inverse is not None:
        specs.append(whole(inverse.shape))
    return pl.pallas_call(
        functools.partial(sketch_kernel, masks, inverse is not None),
        out_shape=[jax.ShapeDtypeStruct(near.shape, F32), jax.ShapeDtypeStruct(near.shape, BF16)],
        grid_spec=pltpu.PrefetchScalarGridSpec(
            num_scalar_prefetch=1,
            grid=(rows // tile,),
            in_specs=specs,
            out_specs=[whole(near.shape), whole(near.shape)],
            scratch_shapes=[
                pltpu.VMEM((features, rank), BF16),
                pltpu.VMEM((rank, features), F32),
                pltpu.VMEM((features, rank), F32),
            ],
        ),
        compiler_params=pltpu.CompilerParams(dimension_semantics=("arbitrary",), vmem_limit_bytes=40 << 20),
        name="sketch",
    )(me, *given)


def project_kernel(masks, me_ref, a_ref, near_ref, far_ref, inv_ref, out_ref, full_ref):
    @pl.when(pl.program_id(0) == 0)
    def _():
        assemble(masks, me_ref[0], near_ref, far_ref, full_ref)

    image = jnp.dot(a_ref[...], full_ref[...], preferred_element_type=F32)
    image = jnp.dot(image, inv_ref[...], precision=lax.Precision.HIGHEST, preferred_element_type=F32)
    out_ref[...] = image.astype(BF16)


def project_call(masks, me, a, near, far, inverse):
    rows, features = a.shape
    slots, block, rank = near.shape
    tile = row_tile(rows)
    whole = lambda shape: pl.BlockSpec(shape, lambda i, *_: (0,) * len(shape))
    return pl.pallas_call(
        functools.partial(project_kernel, masks),
        out_shape=jax.ShapeDtypeStruct((rows, rank), BF16),
        grid_spec=pltpu.PrefetchScalarGridSpec(
            num_scalar_prefetch=1,
            grid=(rows // tile,),
            in_specs=[
                pl.BlockSpec((tile, features), lambda i, *_: (i, 0)),
                whole(near.shape),
                whole(far.shape),
                whole(inverse.shape),
            ],
            out_specs=pl.BlockSpec((tile, rank), lambda i, *_: (i, 0)),
            scratch_shapes=[pltpu.VMEM((features, rank), BF16)],
        ),
        compiler_params=pltpu.CompilerParams(dimension_semantics=("arbitrary",), vmem_limit_bytes=40 << 20),
        name="project",
    )(me, a, near, far, inverse)


def gram_of(x):
    x = x.reshape(-1, x.shape[-1])
    return lax.dot_general(x, x, (((0,), (0,)), ((), ())), preferred_element_type=F32)


def inverse_factor(near, far):
    gram = gram_of(near) + gram_of(far)
    lower = jnp.linalg.cholesky(gram)
    eye = jnp.eye(gram.shape[0], dtype=F32)
    return jax.scipy.linalg.solve_triangular(lower, eye, lower=True).T


def solution(mesh):
    plan = Plan(mesh)

    def body(sample_rows, start_basis):
        features = sample_rows.shape[1]
        me = lax.axis_index(plan.axes).astype(jnp.int32).reshape(1)
        near, far = plan.all_gather(start_basis)
        inverse = None
        for _ in range(ITERS):
            own, other = sketch_call(plan.masks, me, sample_rows, near, far, inverse)
            mine = plan.reduce_scatter(own, other)
            near, far = plan.all_gather(mine.astype(BF16))
            inverse = inverse_factor(near, far)
        projected = project_call(plan.masks, me, sample_rows, near, far, inverse)
        ortho = jnp.dot(mine, inverse, precision=lax.Precision.HIGHEST, preferred_element_type=F32)
        return projected, ortho * math.sqrt(features)

    spec = P(plan.axes, None)
    return jax.shard_map(body, mesh=mesh, in_specs=(spec, spec), out_specs=(spec, spec), check_vma=False)
```

```python
import functools
import math

import jax
import jax.numpy as jnp
from jax import lax
from jax.experimental import pallas as pl
from jax.experimental.pallas import tpu as pltpu
from jax.sharding import PartitionSpec as P

ITERS = 2
F32 = jnp.float32
BF16 = jnp.bfloat16
PANEL = 32


def digits(size, stride):
    found = []
    while size > 1:
        radix = 4 if size % 4 == 0 else 2
        found.append((stride, radix))
        size //= radix
        stride *= radix
    return found


class Plan:
    def __init__(self, mesh):
        self.axes = tuple(mesh.axis_names)
        outer, inner = (mesh.shape[a] for a in self.axes)
        self.n = outer * inner
        assert self.n & (self.n - 1) == 0 and inner % 2 == 0
        self.steps = digits(outer, inner) + digits(inner // 2, 2)[::-1]
        masks = [0]
        for stride, radix in self.steps:
            masks = [m ^ (stride * d) for m in masks for d in range(radix)]
        self.masks = masks

    def swap(self, x, mask):
        return lax.ppermute(x, self.axes, [(i, i ^ mask) for i in range(self.n)])

    def reduce_scatter(self, own, other):
        total = own + self.swap(other, 1).astype(F32)
        for stride, radix in self.steps:
            parts = total.reshape((radix, -1) + total.shape[1:])
            received = [self.swap(parts[d].astype(BF16), stride * d) for d in range(1, radix)]
            total = parts[0]
            for r in received:
                total = total + r.astype(F32)
        return total[0]

    def all_gather(self, block):
        have = block[None]
        for stride, radix in self.steps[::-1]:
            have = jnp.concatenate([have] + [self.swap(have, stride * d) for d in range(1, radix)], 0)
        return have, self.swap(have, 1)


def row_tile(rows):
    return 256 if rows % 256 == 0 else rows


def assemble(masks, me, near_ref, far_ref, full_ref):
    block = near_ref.shape[1]
    for slot, mask in enumerate(masks):
        at = jnp.bitwise_xor(me, mask)
        full_ref[pl.ds(pl.multiple_of(at * block, block), block), :] = near_ref[slot]
        at = jnp.bitwise_xor(me, mask ^ 1)
        full_ref[pl.ds(pl.multiple_of(at * block, block), block), :] = far_ref[slot]


def sketch_kernel(masks, scaled, me_ref, a_ref, near_ref, far_ref, *refs):
    if scaled:
        inv_ref, own_ref, other_ref, full_ref, acc_ref, turned_ref = refs
    else:
        own_ref, other_ref, full_ref, acc_ref, turned_ref = refs
    step = pl.program_id(0)
    me = me_ref[0]

    @pl.when(step == 0)
    def _():
        assemble(masks, me, near_ref, far_ref, full_ref)

    tile = a_ref[...]
    image = jnp.dot(tile, full_ref[...], preferred_element_type=F32)
    if scaled:
        image = jnp.dot(image, inv_ref[...], precision=lax.Precision.HIGHEST, preferred_element_type=F32)
    low = image.astype(BF16)
    term = lax.dot_general(low, tile, (((0,), (0,)), ((), ())), preferred_element_type=F32)

    @pl.when(step == 0)
    def _():
        acc_ref[...] = term

    @pl.when(step > 0)
    def _():
        acc_ref[...] += term

    @pl.when(step == pl.num_programs(0) - 1)
    def _():
        turned_ref[...] = acc_ref[...].T
        block = own_ref.shape[1]
        for slot, mask in enumerate(masks):
            at = jnp.bitwise_xor(me, mask)
            own_ref[slot] = turned_ref[pl.ds(pl.multiple_of(at * block, block), block), :]
            at = jnp.bitwise_xor(me, mask ^ 1)
            other_ref[slot] = turned_ref[pl.ds(pl.multiple_of(at * block, block), block), :].astype(BF16)


def sketch_call(masks, me, a, near, far, inverse=None):
    rows, features = a.shape
    slots, block, rank = near.shape
    tile = row_tile(rows)
    whole = lambda shape: pl.BlockSpec(shape, lambda i, *_: (0,) * len(shape))
    given = [a, near, far] + ([] if inverse is None else [inverse])
    specs = [pl.BlockSpec((tile, features), lambda i, *_: (i, 0)), whole(near.shape), whole(far.shape)]
    if inverse is not None:
        specs.append(whole(inverse.shape))
    return pl.pallas_call(
        functools.partial(sketch_kernel, masks, inverse is not None),
        out_shape=[jax.ShapeDtypeStruct(near.shape, F32), jax.ShapeDtypeStruct(near.shape, BF16)],
        grid_spec=pltpu.PrefetchScalarGridSpec(
            num_scalar_prefetch=1,
            grid=(rows // tile,),
            in_specs=specs,
            out_specs=[whole(near.shape), whole(near.shape)],
            scratch_shapes=[
                pltpu.VMEM((features, rank), BF16),
                pltpu.VMEM((rank, features), F32),
                pltpu.VMEM((features, rank), F32),
            ],
        ),
        compiler_params=pltpu.CompilerParams(dimension_semantics=("arbitrary",), vmem_limit_bytes=40 << 20),
        name="sketch",
    )(me, *given)


def project_kernel(masks, me_ref, a_ref, near_ref, far_ref, inv_ref, out_ref, full_ref):
    @pl.when(pl.program_id(0) == 0)
    def _():
        assemble(masks, me_ref[0], near_ref, far_ref, full_ref)

    image = jnp.dot(a_ref[...], full_ref[...], preferred_element_type=F32)
    image = jnp.dot(image, inv_ref[...], precision=lax.Precision.HIGHEST, preferred_element_type=F32)
    out_ref[...] = image.astype(BF16)


def project_call(masks, me, a, near, far, inverse):
    rows, features = a.shape
    slots, block, rank = near.shape
    tile = row_tile(rows)
    whole = lambda shape: pl.BlockSpec(shape, lambda i, *_: (0,) * len(shape))
    return pl.pallas_call(
        functools.partial(project_kernel, masks),
        out_shape=jax.ShapeDtypeStruct((rows, rank), BF16),
        grid_spec=pltpu.PrefetchScalarGridSpec(
            num_scalar_prefetch=1,
            grid=(rows // tile,),
            in_specs=[
                pl.BlockSpec((tile, features), lambda i, *_: (i, 0)),
                whole(near.shape),
                whole(far.shape),
                whole(inverse.shape),
            ],
            out_specs=pl.BlockSpec((tile, rank), lambda i, *_: (i, 0)),
            scratch_shapes=[pltpu.VMEM((features, rank), BF16)],
        ),
        compiler_params=pltpu.CompilerParams(dimension_semantics=("arbitrary",), vmem_limit_bytes=40 << 20),
        name="project",
    )(me, a, near, far, inverse)


def turned_dot(x, y, precision=None):
    return lax.dot_general(x, y, (((0,), (0,)), ((), ())), precision=precision, preferred_element_type=F32)


def eliminate(left, right, first, size):
    row = lax.broadcasted_iota(jnp.int32, left[0].shape, 0)
    spread = lambda x, j: jnp.broadcast_to(x[j : j + 1, :], x.shape)
    for g in range(size // 8):
        columns = [
            [jnp.broadcast_to(left[h][:, c : c + 1], left[h].shape) for c in range(first + 8 * g, first + 8 * g + 8)]
            for h in range(g, size // 8)
        ]
        scale = jnp.zeros_like(left[g])
        for j in range(8):
            pivot = spread(columns[0][j], j)
            root = lax.rsqrt(pivot)
            root = root * (1.5 - 0.5 * pivot * root * root)
            weight = root * root
            scale = jnp.where(row == j, root, scale)
            pivots = [None if k <= j else spread(columns[0][k], j) for k in range(8)]
            left_row, right_row = spread(left[g], j), spread(right[g], j)
            for h in range(g, size // 8):
                own = columns[h - g]
                factor = own[j] * weight
                if h == g:
                    factor = jnp.where(row > j, factor, 0.0)
                for k in range(j + 1, 8):
                    own[k] = own[k] - factor * pivots[k]
                left[h] = left[h] - factor * left_row
                right[h] = right[h] - factor * right_row
        left[g] = left[g] * scale
        right[g] = right[g] * scale


def factor_kernel(panel, near_ref, far_ref, inv_ref):
    flat = lambda ref: ref[...].reshape(-1, ref.shape[-1])
    near, far = flat(near_ref), flat(far_ref)
    gram = turned_dot(near, near) + turned_dot(far, far)
    rank = gram.shape[0]
    shape = gram.shape
    eye = (lax.broadcasted_iota(jnp.int32, shape, 0) == lax.broadcasted_iota(jnp.int32, shape, 1)).astype(F32)
    rest_left, rest_right, done = gram, eye, []
    for first in range(0, rank, panel):
        groups = lambda x: [x[i : i + 8, :] for i in range(0, panel, 8)]
        left, right = groups(rest_left), groups(rest_right)
        eliminate(left, right, first, panel)
        left, right = jnp.concatenate(left, 0), jnp.concatenate(right, 0)
        done.append(right)
        if first + panel < rank:
            below = left[:, first + panel :]
            high = lax.Precision.HIGHEST
            rest_left = rest_left[panel:] - turned_dot(below, left, high)
            rest_right = rest_right[panel:] - turned_dot(below, right, high)
    inv_ref[...] = jnp.concatenate(done, 0).T


def inverse_factor(near, far):
    rank = near.shape[-1]
    panel = next(p for p in (PANEL, 16, 8) if rank % p == 0)
    return pl.pallas_call(
        functools.partial(factor_kernel, panel),
        out_shape=jax.ShapeDtypeStruct((rank, rank), F32),
        in_specs=[pl.BlockSpec(memory_space=pltpu.VMEM)] * 2,
        out_specs=pl.BlockSpec(memory_space=pltpu.VMEM),
        compiler_params=pltpu.CompilerParams(vmem_limit_bytes=16 << 20),
        name="factor",
    )(near, far)


def solution(mesh):
    plan = Plan(mesh)

    def body(sample_rows, start_basis):
        features = sample_rows.shape[1]
        me = lax.axis_index(plan.axes).astype(jnp.int32).reshape(1)
        near, far = plan.all_gather(start_basis)
        inverse = None
        for _ in range(ITERS):
            own, other = sketch_call(plan.masks, me, sample_rows, near, far, inverse)
            mine = plan.reduce_scatter(own, other)
            near, far = plan.all_gather(mine.astype(BF16))
            inverse = inverse_factor(near, far)
        projected = project_call(plan.masks, me, sample_rows, near, far, inverse)
        ortho = jnp.dot(mine, inverse, precision=lax.Precision.HIGHEST, preferred_element_type=F32)
        return projected, ortho * math.sqrt(features)

    spec = P(plan.axes, None)
    return jax.shard_map(body, mesh=mesh, in_specs=(spec, spec), out_specs=(spec, spec), check_vma=False)
```

```python
import functools
import itertools
import math

import jax
import jax.numpy as jnp
from jax import lax
from jax.experimental import pallas as pl
from jax.experimental.pallas import tpu as pltpu
from jax.sharding import PartitionSpec as P

ITERS = 2
F32 = jnp.float32
BF16 = jnp.bfloat16
PANEL = 32


def digits(size, stride):
    found = []
    while size > 1:
        radix = 4 if size % 4 == 0 else 2
        found.append((stride, radix))
        size //= radix
        stride *= radix
    return found


class Plan:
    def __init__(self, mesh):
        self.axes = tuple(mesh.axis_names)
        outer, inner = (mesh.shape[a] for a in self.axes)
        self.n = outer * inner
        assert self.n & (self.n - 1) == 0 and inner % 2 == 0
        self.steps = [(s, r, False) for s, r in digits(outer, inner)]
        self.steps += [(s, r, True) for s, r in digits(inner // 2, 2)[::-1]]
        self.slots = list(itertools.product(*[range(r) for _, r, _ in self.steps]))

    def partner(self, index, step, d):
        stride, radix, cyclic = step
        if not cyclic:
            return index ^ (stride * d)
        digit = (index >> (stride.bit_length() - 1)) & (radix - 1)
        return index + (((digit + d) & (radix - 1)) - digit) * stride

    def owners(self, me):
        found = []
        for slot in self.slots:
            at = me
            for step, d in zip(self.steps, slot):
                at = self.partner(at, step, d) if d else at
            found.append(at)
        return found

    def swap(self, x, step, d):
        return lax.ppermute(x, self.axes, [(i, self.partner(i, step, d)) for i in range(self.n)])

    def other_core(self, x):
        return self.swap(x, (1, 2, False), 1)

    def reduce_scatter(self, own, other):
        total = own + self.other_core(other).astype(F32)
        for step in self.steps:
            radix = step[1]
            parts = total.reshape((radix, -1) + total.shape[1:])
            received = [self.swap(parts[d].astype(BF16), step, d) for d in range(1, radix)]
            total = parts[0]
            for r in received:
                total = total + r.astype(F32)
        return total[0]

    def all_gather(self, block):
        have = block[None]
        for step in self.steps[::-1]:
            radix = step[1]
            back = lambda d: radix - d if step[2] else d
            have = jnp.concatenate([have] + [self.swap(have, step, back(d)) for d in range(1, radix)], 0)
        return have, self.other_core(have)


def row_tile(rows):
    return 256 if rows % 256 == 0 else rows


def rows_of(at, block):
    return pl.ds(pl.multiple_of(at * block, block), block)


def assemble(plan, me, near_ref, far_ref, full_ref):
    block = near_ref.shape[1]
    for slot, at in enumerate(plan.owners(me)):
        full_ref[rows_of(at, block), :] = near_ref[slot]
        full_ref[rows_of(at ^ 1, block), :] = far_ref[slot]


def scaled_dot(x, inverse):
    high, inverse_high = x.astype(BF16), inverse.astype(BF16)
    low, inverse_low = (x - high.astype(F32)).astype(BF16), (inverse - inverse_high.astype(F32)).astype(BF16)
    dot = functools.partial(jnp.dot, preferred_element_type=F32)
    both = dot(jnp.concatenate([high, low], 1), jnp.concatenate([inverse_high, inverse_high], 0))
    return both + dot(jnp.concatenate([high, low], 1), jnp.concatenate([inverse_low, inverse_low], 0))


def turned_dot(x, y, precision=None):
    return lax.dot_general(x, y, (((0,), (0,)), ((), ())), precision=precision, preferred_element_type=F32)


def eliminate(left, right, first, size):
    row = lax.broadcasted_iota(jnp.int32, left[0].shape, 0)
    spread = lambda x, j: jnp.broadcast_to(x[j : j + 1, :], x.shape)
    for g in range(size // 8):
        columns = [
            [jnp.broadcast_to(left[h][:, c : c + 1], left[h].shape) for c in range(first + 8 * g, first + 8 * g + 8)]
            for h in range(g, size // 8)
        ]
        scale = jnp.zeros_like(left[g])
        for j in range(8):
            pivot = spread(columns[0][j], j)
            root = lax.rsqrt(pivot)
            root = root * (1.5 - 0.5 * pivot * root * root)
            weight = root * root
            scale = jnp.where(row == j, root, scale)
            pivots = [None if k <= j else spread(columns[0][k], j) for k in range(8)]
            left_row, right_row = spread(left[g], j), spread(right[g], j)
            for h in range(g, size // 8):
                own = columns[h - g]
                factor = own[j] * weight
                if h == g:
                    factor = jnp.where(row > j, factor, 0.0)
                for k in range(j + 1, 8):
                    own[k] = own[k] - factor * pivots[k]
                left[h] = left[h] - factor * left_row
                right[h] = right[h] - factor * right_row
        left[g] = left[g] * scale
        right[g] = right[g] * scale


def put_sketch(plan, me, acc_ref, turned_ref, own_ref, other_ref):
    turned_ref[...] = acc_ref[...].T
    block = own_ref.shape[1]
    for slot, at in enumerate(plan.owners(me)):
        own_ref[slot] = turned_ref[rows_of(at, block), :]
        other_ref[slot] = turned_ref[rows_of(at ^ 1, block), :].astype(BF16)


def add_term(first, acc_ref, low, tile):
    term = turned_dot(low, tile)

    @pl.when(first)
    def _():
        acc_ref[...] = term

    @pl.when(jnp.logical_not(first))
    def _():
        acc_ref[...] += term


def first_kernel(plan, me_ref, a_ref, near_ref, far_ref, own_ref, other_ref, full_ref, acc_ref, turned_ref):
    step = pl.program_id(0)

    @pl.when(step == 0)
    def _():
        assemble(plan, me_ref[0], near_ref, far_ref, full_ref)

    tile = a_ref[...]
    low = jnp.dot(tile, full_ref[...], preferred_element_type=F32).astype(BF16)
    add_term(step == 0, acc_ref, low, tile)

    @pl.when(step == pl.num_programs(0) - 1)
    def _():
        put_sketch(plan, me_ref[0], acc_ref, turned_ref, own_ref, other_ref)


def factor_and_image(plan, step, me_ref, a_ref, near_ref, far_ref, full_ref, image_ref, left_ref, right_ref, inv_ref):
    rank = full_ref.shape[1]

    @pl.when(step == 0)
    def _():
        assemble(plan, me_ref[0], near_ref, far_ref, full_ref)
        full = full_ref[...]
        left_ref[...] = turned_dot(full, full)
        shape = (rank, rank)
        eye = lax.broadcasted_iota(jnp.int32, shape, 0) == lax.broadcasted_iota(jnp.int32, shape, 1)
        right_ref[...] = eye.astype(F32)

    tile = a_ref.shape[0]
    for index, start in enumerate(range(0, rank, PANEL)):

        @pl.when(step == index)
        def _(index=index, start=start):
            end = start + PANEL
            groups = lambda ref: [ref[i : i + 8, :] for i in range(start, end, 8)]
            left, right = groups(left_ref), groups(right_ref)
            image = jnp.dot(a_ref[...], full_ref[...], preferred_element_type=F32)
            eliminate(left, right, start, PANEL)
            left, right = jnp.concatenate(left, 0), jnp.concatenate(right, 0)
            image_ref[index * tile : (index + 1) * tile, :] = image
            right_ref[start:end, :] = right
            if end < rank:
                below = left[:, end:]
                high = lax.Precision.HIGHEST
                left_ref[end:, :] -= turned_dot(below, left, high)
                right_ref[end:, :] -= turned_dot(below, right, high)
            else:
                inv_ref[...] = right_ref[...].T


def next_kernel(plan, tiles, me_ref, a_ref, near_ref, far_ref, own_ref, other_ref, acc_ref, turned_ref, *refs):
    step = pl.program_id(0)
    factor_and_image(plan, step, me_ref, a_ref, near_ref, far_ref, *refs)
    image_ref, inv_ref = refs[1], refs[4]

    @pl.when(step >= tiles)
    def _():
        tile = a_ref[...]
        rows = tile.shape[0]
        image = image_ref[rows_of(step - tiles, rows), :]
        add_term(step == tiles, acc_ref, scaled_dot(image, inv_ref[...]).astype(BF16), tile)

    @pl.when(step == pl.num_programs(0) - 1)
    def _():
        put_sketch(plan, me_ref[0], acc_ref, turned_ref, own_ref, other_ref)


def last_kernel(plan, tiles, me_ref, a_ref, near_ref, far_ref, mine_ref, projected_ref, basis_ref, *refs):
    step = pl.program_id(0)
    factor_and_image(plan, step, me_ref, a_ref, near_ref, far_ref, *refs)
    image_ref, inv_ref = refs[1], refs[4]

    @pl.when(step == tiles)
    def _():
        inverse = inv_ref[...]
        projected_ref[...] = scaled_dot(image_ref[...], inverse).astype(BF16)
        ortho = jnp.dot(mine_ref[...], inverse, precision=lax.Precision.HIGHEST, preferred_element_type=F32)
        basis_ref[...] = ortho * math.sqrt(a_ref.shape[1])


def call(kernel, name, steps, tiles, a, whole_args, outs, scratch, me):
    rows, features = a.shape
    whole = lambda shape: pl.BlockSpec(shape, lambda i, *_: (0,) * len(shape))
    where = lambda i, *_: (jnp.minimum(i, tiles - 1) if steps == tiles + 1 else lax.rem(i, tiles), 0)
    return pl.pallas_call(
        kernel,
        out_shape=outs,
        grid_spec=pltpu.PrefetchScalarGridSpec(
            num_scalar_prefetch=1,
            grid=(steps,),
            in_specs=[pl.BlockSpec((rows // tiles, features), where)] + [whole(x.shape) for x in whole_args],
            out_specs=[whole(o.shape) for o in outs],
            scratch_shapes=scratch,
        ),
        compiler_params=pltpu.CompilerParams(dimension_semantics=("arbitrary",), vmem_limit_bytes=56 << 20),
        name=name,
    )(me, a, *whole_args)


def solution(mesh):
    plan = Plan(mesh)

    def body(sample_rows, start_basis):
        rows, features = sample_rows.shape
        block, rank = start_basis.shape
        panels = rank // PANEL
        assert rank % PANEL == 0 and rows % (8 * panels) == 0
        me = lax.axis_index(plan.axes).astype(jnp.int32).reshape(1)
        halves = (plan.n // 2, block, rank)
        sketch = [jax.ShapeDtypeStruct(halves, F32), jax.ShapeDtypeStruct(halves, BF16)]
        full = pltpu.VMEM((features, rank), BF16)
        sums = [pltpu.VMEM((rank, features), F32), pltpu.VMEM((features, rank), F32)]
        square = pltpu.VMEM((rank, rank), F32)
        factors = [full, pltpu.VMEM((rows, rank), F32), square, square, square]

        tiles = rows // row_tile(rows)
        near, far = plan.all_gather(start_basis)
        kernel = functools.partial(first_kernel, plan)
        own, other = call(kernel, "first", tiles, tiles, sample_rows, [near, far], sketch, [full] + sums, me)
        for _ in range(ITERS - 1):
            near, far = plan.all_gather(plan.reduce_scatter(own, other).astype(BF16))
            kernel = functools.partial(next_kernel, plan, panels)
            own, other = call(
                kernel, "next", 2 * panels, panels, sample_rows, [near, far], sketch, sums + factors, me
            )
        mine = plan.reduce_scatter(own, other)
        near, far = plan.all_gather(mine.astype(BF16))
        kernel = functools.partial(last_kernel, plan, panels)
        outs = [jax.ShapeDtypeStruct((rows, rank), BF16), jax.ShapeDtypeStruct((block, rank), F32)]
        return tuple(call(kernel, "last", panels + 1, panels, sample_rows, [near, far, mine], outs, factors, me))

    spec = P(plan.axes, None)
    return jax.shard_map(body, mesh=mesh, in_specs=(spec, spec), out_specs=(spec, spec), check_vma=False)
```

```python
import functools
import itertools
import math

import jax
import jax.numpy as jnp
from jax import lax
from jax.experimental import pallas as pl
from jax.experimental.pallas import tpu as pltpu
from jax.sharding import PartitionSpec as P

ITERS = 2
F32 = jnp.float32
BF16 = jnp.bfloat16
PANEL = 32


def digits(size, stride):
    found = []
    while size > 1:
        radix = 4 if size % 4 == 0 else 2
        found.append((stride, radix))
        size //= radix
        stride *= radix
    return found


class Plan:
    def __init__(self, mesh):
        self.axes = tuple(mesh.axis_names)
        outer, inner = (mesh.shape[a] for a in self.axes)
        self.n = outer * inner
        assert self.n & (self.n - 1) == 0 and inner % 2 == 0
        self.steps = [(s, r, False) for s, r in digits(outer, inner)]
        self.steps += [(s, r, True) for s, r in digits(inner // 2, 2)[::-1]]
        self.slots = list(itertools.product(*[range(r) for _, r, _ in self.steps]))

    def partner(self, index, step, d):
        stride, radix, cyclic = step
        if not cyclic:
            return index ^ (stride * d)
        digit = (index >> (stride.bit_length() - 1)) & (radix - 1)
        return index + (((digit + d) & (radix - 1)) - digit) * stride

    def owners(self, me):
        found = []
        for slot in self.slots:
            at = me
            for step, d in zip(self.steps, slot):
                at = self.partner(at, step, d) if d else at
            found.append(at)
        return found

    def swap(self, x, step, d):
        return lax.ppermute(x, self.axes, [(i, self.partner(i, step, d)) for i in range(self.n)])

    def other_core(self, x):
        return self.swap(x, (1, 2, False), 1)

    def reduce_scatter(self, own, other):
        total = own + self.other_core(other).astype(F32)
        for step in self.steps:
            radix = step[1]
            parts = total.reshape((radix, -1) + total.shape[1:])
            received = [self.swap(parts[d].astype(BF16), step, d) for d in range(1, radix)]
            total = parts[0]
            for r in received:
                total = total + r.astype(F32)
        return total[0]

    def all_gather(self, block):
        have = block[None]
        for step in self.steps[::-1]:
            radix = step[1]
            back = lambda d: radix - d if step[2] else d
            have = jnp.concatenate([have] + [self.swap(have, step, back(d)) for d in range(1, radix)], 0)
        return have, self.other_core(have)


def row_tile(rows):
    return 256 if rows % 256 == 0 else rows


def rows_of(at, block):
    return pl.ds(pl.multiple_of(at * block, block), block)


def assemble(plan, me, near_ref, far_ref, full_ref):
    block = near_ref.shape[1]
    for slot, at in enumerate(plan.owners(me)):
        full_ref[rows_of(at, block), :] = near_ref[slot]
        full_ref[rows_of(at ^ 1, block), :] = far_ref[slot]


def scaled_dot(x, inverse):
    high, inverse_high = x.astype(BF16), inverse.astype(BF16)
    low, inverse_low = (x - high.astype(F32)).astype(BF16), (inverse - inverse_high.astype(F32)).astype(BF16)
    dot = functools.partial(jnp.dot, preferred_element_type=F32)
    both = dot(jnp.concatenate([high, low], 1), jnp.concatenate([inverse_high, inverse_high], 0))
    return both + dot(jnp.concatenate([high, low], 1), jnp.concatenate([inverse_low, inverse_low], 0))


def turned_dot(x, y, precision=None):
    return lax.dot_general(x, y, (((0,), (0,)), ((), ())), precision=precision, preferred_element_type=F32)


def eliminate(left, right, first, size):
    row = lax.broadcasted_iota(jnp.int32, left[0].shape, 0)
    spread = lambda x, j: jnp.broadcast_to(x[j : j + 1, :], x.shape)
    for g in range(size // 8):
        columns = [
            [jnp.broadcast_to(left[h][:, c : c + 1], left[h].shape) for c in range(first + 8 * g, first + 8 * g + 8)]
            for h in range(g, size // 8)
        ]
        scale = jnp.zeros_like(left[g])
        for j in range(8):
            pivot = spread(columns[0][j], j)
            root = lax.rsqrt(pivot)
            root = root * (1.5 - 0.5 * pivot * root * root)
            weight = root * root
            scale = jnp.where(row == j, root, scale)
            pivots = [None if k <= j else spread(columns[0][k], j) for k in range(8)]
            left_row, right_row = spread(left[g], j), spread(right[g], j)
            for h in range(g, size // 8):
                own = columns[h - g]
                factor = own[j] * weight
                if h == g:
                    factor = jnp.where(row > j, factor, 0.0)
                for k in range(j + 1, 8):
                    own[k] = own[k] - factor * pivots[k]
                left[h] = left[h] - factor * left_row
                right[h] = right[h] - factor * right_row
        left[g] = left[g] * scale
        right[g] = right[g] * scale


def put_sketch(plan, me, acc_ref, turned_ref, own_ref, other_ref):
    turned_ref[...] = acc_ref[...].T
    block = own_ref.shape[1]
    for slot, at in enumerate(plan.owners(me)):
        own_ref[slot] = turned_ref[rows_of(at, block), :]
        other_ref[slot] = turned_ref[rows_of(at ^ 1, block), :].astype(BF16)


def add_term(first, acc_ref, low, tile):
    term = turned_dot(low, tile)

    @pl.when(first)
    def _():
        acc_ref[...] = term

    @pl.when(jnp.logical_not(first))
    def _():
        acc_ref[...] += term


def first_kernel(plan, me_ref, a_ref, near_ref, far_ref, own_ref, other_ref, full_ref, acc_ref, turned_ref):
    step = pl.program_id(0)

    @pl.when(step == 0)
    def _():
        assemble(plan, me_ref[0], near_ref, far_ref, full_ref)

    tile = a_ref[...]
    low = jnp.dot(tile, full_ref[...], preferred_element_type=F32).astype(BF16)
    add_term(step == 0, acc_ref, low, tile)

    @pl.when(step == pl.num_programs(0) - 1)
    def _():
        put_sketch(plan, me_ref[0], acc_ref, turned_ref, own_ref, other_ref)


def factor_and_image(plan, step, me_ref, a_ref, near_ref, far_ref, full_ref, image_ref, left_ref, right_ref, inv_ref):
    rank = full_ref.shape[1]

    @pl.when(step == 0)
    def _():
        assemble(plan, me_ref[0], near_ref, far_ref, full_ref)
        full = full_ref[...]
        left_ref[...] = turned_dot(full, full)
        shape = (rank, rank)
        eye = lax.broadcasted_iota(jnp.int32, shape, 0) == lax.broadcasted_iota(jnp.int32, shape, 1)
        right_ref[...] = eye.astype(F32)

    tile = a_ref.shape[0]
    for index, start in enumerate(range(0, rank, PANEL)):

        @pl.when(step == index)
        def _(index=index, start=start):
            end = start + PANEL
            groups = lambda ref: [ref[i : i + 8, :] for i in range(start, end, 8)]
            left, right = groups(left_ref), groups(right_ref)
            image = jnp.dot(a_ref[...], full_ref[...], preferred_element_type=F32)
            eliminate(left, right, start, PANEL)
            left, right = jnp.concatenate(left, 0), jnp.concatenate(right, 0)
            image_ref[index * tile : (index + 1) * tile, :] = image
            right_ref[start:end, :] = right
            if end < rank:
                below = left[:, end:]
                high = lax.Precision.HIGHEST
                left_ref[end:, :] -= turned_dot(below, left, high)
                right_ref[end:, :] -= turned_dot(below, right, high)
            else:
                inv_ref[...] = right_ref[...].T


def next_kernel(plan, tiles, me_ref, a_ref, near_ref, far_ref, own_ref, other_ref, acc_ref, turned_ref, *refs):
    step = pl.program_id(0)
    factor_and_image(plan, step, me_ref, a_ref, near_ref, far_ref, *refs)
    image_ref, inv_ref = refs[1], refs[4]

    @pl.when(step >= tiles)
    def _():
        tile = a_ref[...]
        rows = tile.shape[0]
        image = image_ref[rows_of(step - tiles, rows), :]
        add_term(step == tiles, acc_ref, scaled_dot(image, inv_ref[...]).astype(BF16), tile)

    @pl.when(step == pl.num_programs(0) - 1)
    def _():
        put_sketch(plan, me_ref[0], acc_ref, turned_ref, own_ref, other_ref)


def last_kernel(plan, tiles, me_ref, a_ref, near_ref, far_ref, mine_ref, projected_ref, basis_ref, *refs):
    step = pl.program_id(0)
    factor_and_image(plan, step, me_ref, a_ref, near_ref, far_ref, *refs)
    image_ref, inv_ref = refs[1], refs[4]

    @pl.when(step == tiles)
    def _():
        inverse = inv_ref[...]
        projected_ref[...] = scaled_dot(image_ref[...], inverse).astype(BF16)
        ortho = jnp.dot(mine_ref[...], inverse, precision=lax.Precision.HIGHEST, preferred_element_type=F32)
        basis_ref[...] = ortho * math.sqrt(a_ref.shape[1])


def call(kernel, name, steps, tiles, a, whole_args, outs, scratch, me, limit):
    rows, features = a.shape
    whole = lambda shape: pl.BlockSpec(shape, lambda i, *_: (0,) * len(shape))
    where = lambda i, *_: (jnp.minimum(i, tiles - 1) if steps == tiles + 1 else lax.rem(i, tiles), 0)
    return pl.pallas_call(
        kernel,
        out_shape=outs,
        grid_spec=pltpu.PrefetchScalarGridSpec(
            num_scalar_prefetch=1,
            grid=(steps,),
            in_specs=[pl.BlockSpec((rows // tiles, features), where)] + [whole(x.shape) for x in whole_args],
            out_specs=[whole(o.shape) for o in outs],
            scratch_shapes=scratch,
        ),
        compiler_params=pltpu.CompilerParams(dimension_semantics=("arbitrary",), vmem_limit_bytes=limit << 20),
        name=name,
    )(me, a, *whole_args)


def solution(mesh):
    plan = Plan(mesh)

    def body(sample_rows, start_basis):
        rows, features = sample_rows.shape
        block, rank = start_basis.shape
        panels = rank // PANEL
        assert rank % PANEL == 0 and rows % (8 * panels) == 0
        me = lax.axis_index(plan.axes).astype(jnp.int32).reshape(1)
        halves = (plan.n // 2, block, rank)
        sketch = [jax.ShapeDtypeStruct(halves, F32), jax.ShapeDtypeStruct(halves, BF16)]
        full = pltpu.VMEM((features, rank), BF16)
        sums = [pltpu.VMEM((rank, features), F32), pltpu.VMEM((features, rank), F32)]
        square = pltpu.VMEM((rank, rank), F32)
        factors = [full, pltpu.VMEM((rows, rank), F32), square, square, square]

        tiles = rows // row_tile(rows)
        near, far = plan.all_gather(start_basis)
        kernel = functools.partial(first_kernel, plan)
        own, other = call(kernel, "first", tiles, tiles, sample_rows, [near, far], sketch, [full] + sums, me, 32)
        for _ in range(ITERS - 1):
            near, far = plan.all_gather(plan.reduce_scatter(own, other).astype(BF16))
            kernel = functools.partial(next_kernel, plan, panels)
            own, other = call(
                kernel, "next", 2 * panels, panels, sample_rows, [near, far], sketch, sums + factors, me, 32
            )
        mine = plan.reduce_scatter(own, other)
        near, far = plan.all_gather(mine.astype(BF16))
        kernel = functools.partial(last_kernel, plan, panels)
        outs = [jax.ShapeDtypeStruct((rows, rank), BF16), jax.ShapeDtypeStruct((block, rank), F32)]
        return tuple(call(kernel, "last", panels + 1, panels, sample_rows, [near, far, mine], outs, factors, me, 32))

    spec = P(plan.axes, None)
    return jax.shard_map(body, mesh=mesh, in_specs=(spec, spec), out_specs=(spec, spec), check_vma=False)
```

```python
import functools
import itertools
import math

import jax
import jax.numpy as jnp
from jax import lax
from jax.experimental import pallas as pl
from jax.experimental.pallas import tpu as pltpu
from jax.sharding import PartitionSpec as P

ITERS = 2
F32 = jnp.float32
BF16 = jnp.bfloat16
PANEL = 32


def digits(size, stride):
    found = []
    while size > 1:
        radix = 4 if size % 4 == 0 else 2
        found.append((stride, radix))
        size //= radix
        stride *= radix
    return found


class Plan:
    def __init__(self, mesh):
        self.axes = tuple(mesh.axis_names)
        outer, inner = (mesh.shape[a] for a in self.axes)
        self.n = outer * inner
        assert self.n & (self.n - 1) == 0 and inner % 2 == 0
        self.steps = [(s, r, False) for s, r in digits(outer, inner)]
        self.steps += [(s, r, True) for s, r in digits(inner // 2, 2)[::-1]]
        self.slots = list(itertools.product(*[range(r) for _, r, _ in self.steps]))

    def partner(self, index, step, d):
        stride, radix, cyclic = step
        if not cyclic:
            return index ^ (stride * d)
        digit = (index >> (stride.bit_length() - 1)) & (radix - 1)
        return index + (((digit + d) & (radix - 1)) - digit) * stride

    def owners(self, me):
        found = []
        for slot in self.slots:
            at = me
            for step, d in zip(self.steps, slot):
                at = self.partner(at, step, d) if d else at
            found.append(at)
        return found

    def swap(self, x, step, d):
        return lax.ppermute(x, self.axes, [(i, self.partner(i, step, d)) for i in range(self.n)])

    def other_core(self, x):
        return self.swap(x, (1, 2, False), 1)

    def reduce_scatter(self, own, other):
        total = own + self.other_core(other).astype(F32)
        for step in self.steps:
            radix = step[1]
            parts = total.reshape((radix, -1) + total.shape[1:])
            received = [self.swap(parts[d].astype(BF16), step, d) for d in range(1, radix)]
            total = parts[0]
            for r in received:
                total = total + r.astype(F32)
        return total[0]

    def all_gather(self, block):
        have = block[None]
        for step in self.steps[::-1]:
            radix = step[1]
            back = lambda d: radix - d if step[2] else d
            have = jnp.concatenate([have] + [self.swap(have, step, back(d)) for d in range(1, radix)], 0)
        return have, self.other_core(have)


def row_tile(rows):
    return 256 if rows % 256 == 0 else rows


def rows_of(at, block):
    return pl.ds(pl.multiple_of(at * block, block), block)


def assemble(plan, me, near_ref, far_ref, full_ref):
    block = near_ref.shape[1]
    for slot, at in enumerate(plan.owners(me)):
        full_ref[rows_of(at, block), :] = near_ref[slot]
        full_ref[rows_of(at ^ 1, block), :] = far_ref[slot]


def scaled_dot(x, inverse):
    high, inverse_high = x.astype(BF16), inverse.astype(BF16)
    low, inverse_low = (x - high.astype(F32)).astype(BF16), (inverse - inverse_high.astype(F32)).astype(BF16)
    dot = functools.partial(jnp.dot, preferred_element_type=F32)
    both = dot(jnp.concatenate([high, low], 1), jnp.concatenate([inverse_high, inverse_high], 0))
    return both + dot(jnp.concatenate([high, low], 1), jnp.concatenate([inverse_low, inverse_low], 0))


def turned_dot(x, y, precision=None):
    return lax.dot_general(x, y, (((0,), (0,)), ((), ())), precision=precision, preferred_element_type=F32)


def eliminate(left, right, first, size):
    row = lax.broadcasted_iota(jnp.int32, left[0].shape, 0)
    spread = lambda x, j: jnp.broadcast_to(x[j : j + 1, :], x.shape)
    for g in range(size // 8):
        columns = [
            [jnp.broadcast_to(left[h][:, c : c + 1], left[h].shape) for c in range(first + 8 * g, first + 8 * g + 8)]
            for h in range(g, size // 8)
        ]
        scale = jnp.zeros_like(left[g])
        for j in range(8):
            pivot = spread(columns[0][j], j)
            root = lax.rsqrt(pivot)
            root = root * (1.5 - 0.5 * pivot * root * root)
            weight = root * root
            scale = jnp.where(row == j, root, scale)
            pivots = [None if k <= j else spread(columns[0][k], j) for k in range(8)]
            left_row, right_row = spread(left[g], j), spread(right[g], j)
            for h in range(g, size // 8):
                own = columns[h - g]
                factor = own[j] * weight
                if h == g:
                    factor = jnp.where(row > j, factor, 0.0)
                for k in range(j + 1, 8):
                    own[k] = own[k] - factor * pivots[k]
                left[h] = left[h] - factor * left_row
                right[h] = right[h] - factor * right_row
        left[g] = left[g] * scale
        right[g] = right[g] * scale


def put_sketch(plan, me, acc_ref, turned_ref, own_ref, other_ref):
    turned_ref[...] = acc_ref[...].T
    block = own_ref.shape[1]
    for slot, at in enumerate(plan.owners(me)):
        own_ref[slot] = turned_ref[rows_of(at, block), :]
        other_ref[slot] = turned_ref[rows_of(at ^ 1, block), :].astype(BF16)


def add_term(first, acc_ref, low, tile):
    term = turned_dot(low, tile)

    @pl.when(first)
    def _():
        acc_ref[...] = term

    @pl.when(jnp.logical_not(first))
    def _():
        acc_ref[...] += term


def first_kernel(plan, me_ref, a_ref, near_ref, far_ref, own_ref, other_ref, full_ref, acc_ref, turned_ref):
    step = pl.program_id(0)

    @pl.when(step == 0)
    def _():
        assemble(plan, me_ref[0], near_ref, far_ref, full_ref)

    tile = a_ref[...]
    low = jnp.dot(tile, full_ref[...], preferred_element_type=F32).astype(BF16)
    add_term(step == 0, acc_ref, low, tile)

    @pl.when(step == pl.num_programs(0) - 1)
    def _():
        put_sketch(plan, me_ref[0], acc_ref, turned_ref, own_ref, other_ref)


def factor_and_image(plan, step, me_ref, a_ref, near_ref, far_ref, full_ref, image_ref, left_ref, right_ref, inv_ref):
    rank = full_ref.shape[1]

    @pl.when(step == 0)
    def _():
        assemble(plan, me_ref[0], near_ref, far_ref, full_ref)
        full = full_ref[...]
        left_ref[...] = turned_dot(full, full)
        shape = (rank, rank)
        eye = lax.broadcasted_iota(jnp.int32, shape, 0) == lax.broadcasted_iota(jnp.int32, shape, 1)
        right_ref[...] = eye.astype(F32)

    tile = a_ref.shape[0]
    for index, start in enumerate(range(0, rank, PANEL)):

        @pl.when(step == index)
        def _(index=index, start=start):
            end = start + PANEL
            groups = lambda ref: [ref[i : i + 8, :] for i in range(start, end, 8)]
            left, right = groups(left_ref), groups(right_ref)
            image = jnp.dot(a_ref[...], full_ref[...], preferred_element_type=F32)
            eliminate(left, right, start, PANEL)
            left, right = jnp.concatenate(left, 0), jnp.concatenate(right, 0)
            image_ref[index * tile : (index + 1) * tile, :] = image
            right_ref[start:end, :] = right
            if end < rank:
                below = left[:, end:]
                high = lax.Precision.HIGHEST
                left_ref[end:, :] -= turned_dot(below, left, high)
                right_ref[end:, :] -= turned_dot(below, right, high)
            else:
                inv_ref[...] = right_ref[...].T


def next_kernel(plan, tiles, me_ref, a_ref, near_ref, far_ref, own_ref, other_ref, acc_ref, turned_ref, *refs):
    step = pl.program_id(0)
    factor_and_image(plan, step, me_ref, a_ref, near_ref, far_ref, *refs)
    image_ref, inv_ref = refs[1], refs[4]

    @pl.when(step >= tiles)
    def _():
        tile = a_ref[...]
        rows = tile.shape[0]
        image = image_ref[rows_of(step - tiles, rows), :]
        add_term(step == tiles, acc_ref, scaled_dot(image, inv_ref[...]).astype(BF16), tile)

    @pl.when(step == pl.num_programs(0) - 1)
    def _():
        put_sketch(plan, me_ref[0], acc_ref, turned_ref, own_ref, other_ref)


def last_kernel(plan, tiles, me_ref, a_ref, near_ref, far_ref, mine_ref, projected_ref, basis_ref, *refs):
    step = pl.program_id(0)
    factor_and_image(plan, step, me_ref, a_ref, near_ref, far_ref, *refs)
    image_ref, inv_ref = refs[1], refs[4]

    @pl.when(step == tiles)
    def _():
        inverse = inv_ref[...]
        projected_ref[...] = scaled_dot(image_ref[...], inverse).astype(BF16)
        ortho = jnp.dot(mine_ref[...], inverse, precision=lax.Precision.HIGHEST, preferred_element_type=F32)
        basis_ref[...] = ortho * math.sqrt(a_ref.shape[1])


def call(kernel, name, steps, tiles, a, whole_args, outs, scratch, me, limit):
    rows, features = a.shape
    whole = lambda shape: pl.BlockSpec(shape, lambda i, *_: (0,) * len(shape))
    where = lambda i, *_: (jnp.minimum(i, tiles - 1) if steps == tiles + 1 else lax.rem(i, tiles), 0)
    return pl.pallas_call(
        kernel,
        out_shape=outs,
        grid_spec=pltpu.PrefetchScalarGridSpec(
            num_scalar_prefetch=1,
            grid=(steps,),
            in_specs=[pl.BlockSpec((rows // tiles, features), where)] + [whole(x.shape) for x in whole_args],
            out_specs=[whole(o.shape) for o in outs],
            scratch_shapes=scratch,
        ),
        compiler_params=pltpu.CompilerParams(dimension_semantics=("arbitrary",), vmem_limit_bytes=limit << 20),
        name=name,
    )(me, a, *whole_args)


def solution(mesh):
    plan = Plan(mesh)

    def body(sample_rows, start_basis):
        rows, features = sample_rows.shape
        block, rank = start_basis.shape
        panels = rank // PANEL
        assert rank % PANEL == 0 and rows % (8 * panels) == 0
        me = lax.axis_index(plan.axes).astype(jnp.int32).reshape(1)
        halves = (plan.n // 2, block, rank)
        sketch = [jax.ShapeDtypeStruct(halves, F32), jax.ShapeDtypeStruct(halves, BF16)]
        full = pltpu.VMEM((features, rank), BF16)
        sums = [pltpu.VMEM((rank, features), F32), pltpu.VMEM((features, rank), F32)]
        square = pltpu.VMEM((rank, rank), F32)
        factors = [full, pltpu.VMEM((rows, rank), F32), square, square, square]

        tiles = rows // row_tile(rows)
        near, far = plan.all_gather(start_basis)
        kernel = functools.partial(first_kernel, plan)
        own, other = call(kernel, "first", tiles, tiles, sample_rows, [near, far], sketch, [full] + sums, me, 48)
        for _ in range(ITERS - 1):
            near, far = plan.all_gather(plan.reduce_scatter(own, other).astype(BF16))
            kernel = functools.partial(next_kernel, plan, panels)
            own, other = call(
                kernel, "next", 2 * panels, panels, sample_rows, [near, far], sketch, sums + factors, me, 32
            )
        mine = plan.reduce_scatter(own, other)
        near, far = plan.all_gather(mine.astype(BF16))
        kernel = functools.partial(last_kernel, plan, panels)
        outs = [jax.ShapeDtypeStruct((rows, rank), BF16), jax.ShapeDtypeStruct((block, rank), F32)]
        return tuple(call(kernel, "last", panels + 1, panels, sample_rows, [near, far, mine], outs, factors, me, 32))

    spec = P(plan.axes, None)
    return jax.shard_map(body, mesh=mesh, in_specs=(spec, spec), out_specs=(spec, spec), check_vma=False)
```
